32 devices in a mesh: frame: 8 (over z, y), height: 4 (over x, core).
Axes of the slice: x: 2, y: 2, z: 4, core: 2. Of those that a mesh axis runs over, the one named last changes fastest.
Arguments:
- latents: bfloat16 [8, 24, 64, 1152], P('frame', 'height'), may hold values from -30 to 30
- qkv_weight: bfloat16 [2, 1152, 1728], replicated, as said below
- out_weight: bfloat16 [2, 576, 1152], replicated, may hold values from -0.25 to 0.25
Outputs:
- result: bfloat16 [8, 24, 64, 1152], P('frame', 'height')
The draws below stay inside these ranges and needn't reach their ends.
Inputs may be any that keep to these rules, and one draw needn't show every extreme that they name: `qkv_weight`: entries lie within -0.2 to 0.2.
All inputs are finite; a program needn't handle non-finite values.
Results may differ from the reference program's by a relative error of at most 0.0095.
Values may be sent and summed in bfloat16 or wider, within the bound.
No kernel may reach another device: no remote copies, remote signals or barrier semaphores. Data moves between devices by JAX's collectives and lax.ppermute only.
A program may use at most 64 MiB of HBM per device.

```python
import jax
import jax.numpy as jnp
from jax import lax

D = 1152
HEAD_DIM = 72
HEADS = 8
W = 64
INNER = 576
FRAMES = 8
ROWS = 24


def draw_latents(key, part):
    shape_all = (FRAMES, ROWS, W, D)
    noise_draw = jax.random.normal(jax.random.fold_in(key, 11), shape_all, jnp.float32)
    values_all = noise_draw
    return jnp.clip(values_all, -30.0, 30.0).astype(jnp.bfloat16)


def draw_qkv_weight(key, part):
    inner_width = HEADS * HEAD_DIM
    base = jax.random.normal(jax.random.fold_in(key, 21), (2, D, 3 * inner_width), jnp.float32) * D ** (-0.5)
    return jnp.clip(base, -0.2, 0.2).astype(jnp.bfloat16)


def centred(key, dims, width, reach, held_as=jnp.bfloat16):
    array = width * jax.random.normal(key, dims, jnp.float32)
    return jnp.clip(array, min=-reach, max=reach).astype(held_as)


def setup_inputs(seed: int = 0) -> dict:
    key_of = jax.random.split(jax.random.key(seed), 4)
    latents = draw_latents(jax.random.fold_in(key_of[3], 71), 0)
    qkv_weight = draw_qkv_weight(jax.random.fold_in(key_of[3], 71), 0)
    out_weight = centred(key_of[2], (2, INNER, D), INNER ** -0.5, 0.25)
    return dict(latents=latents, qkv_weight=qkv_weight, out_weight=out_weight)


def layer_norm(values):
    values = values.astype(jnp.float32)
    center = values - lax.optimization_barrier(jnp.mean(values, axis=-1, keepdims=True))
    spread = lax.optimization_barrier(jnp.mean(center * center, axis=-1, keepdims=True))
    return (center * lax.rsqrt(spread + 1e-06)).astype(jnp.bfloat16)

def project(tokens, weight):
    normed = layer_norm(tokens)
    flattened = normed.reshape(-1, normed.shape[-1])
    joined = jnp.dot(flattened, weight, preferred_element_type=jnp.float32)
    return joined.astype(jnp.bfloat16).reshape(tokens.shape[:-1] + (weight.shape[1],))

def attend(joined):
    length, batches = (joined.shape[0], joined.shape[1])
    inner_width = joined.shape[2] // 3
    head_count = inner_width // HEAD_DIM
    query_rows = joined[:, :, :inner_width].reshape(length, batches, head_count, HEAD_DIM).astype(jnp.float32)
    key_rows = joined[:, :, inner_width:2 * inner_width].reshape(length, batches, head_count, HEAD_DIM).astype(jnp.float32)
    value_rows = joined[:, :, 2 * inner_width:].reshape(length, batches, head_count, HEAD_DIM).astype(jnp.float32)
    scores = jnp.einsum('lbnd,mbnd->bnlm', query_rows, key_rows) * HEAD_DIM ** (-0.5)
    scores = scores - lax.optimization_barrier(jnp.max(scores, axis=-1, keepdims=True))
    exponent = jnp.exp(scores)
    weights = (exponent / lax.optimization_barrier(jnp.sum(exponent, axis=-1, keepdims=True))).astype(jnp.bfloat16)
    mixture = jnp.einsum('bnlm,mbnd->lbnd', weights.astype(jnp.float32), value_rows)
    return mixture.reshape(length, batches, inner_width).astype(jnp.bfloat16)

def residual(tokens, mixture, weight):
    update = jnp.dot(mixture.reshape(-1, mixture.shape[-1]), weight, preferred_element_type=jnp.float32)
    return (tokens.astype(jnp.float32) + update.reshape(tokens.shape)).astype(jnp.bfloat16)

def reference(latents, qkv_weight, out_weight):
    joined = lax.map(lambda frame_block: project(frame_block, qkv_weight[0]), latents)
    rows_att = lax.map(attend, joined)
    middle = lax.map(lambda paired: residual(paired[0], paired[1], out_weight[0]), (latents, rows_att))
    joined = lax.map(lambda frame_block: project(frame_block, qkv_weight[1]), middle)
    frames_att = lax.map(attend, jnp.transpose(joined, (1, 0, 2, 3)))
    frames_att = jnp.transpose(frames_att, (1, 0, 2, 3))
    return lax.map(lambda paired: residual(paired[0], paired[1], out_weight[1]), (middle, frames_att))
```

```python
import functools

import jax
import jax.numpy as jnp
from jax import lax
from jax.experimental import pallas as pl
from jax.experimental.pallas import tpu as pltpu
from jax.sharding import PartitionSpec as P

HEAD_DIM = 72
LANES = 128
WINDOW = 256


def layer_norm(values):
    values = values.astype(jnp.float32)
    center = values - jnp.mean(values, axis=-1, keepdims=True)
    spread = jnp.mean(center * center, axis=-1, keepdims=True)
    return (center * lax.rsqrt(spread + 1e-06)).astype(jnp.bfloat16)


def project(tokens, weight):
    normed = layer_norm(tokens)
    flattened = normed.reshape(-1, normed.shape[-1])
    joined = jnp.dot(flattened, weight, preferred_element_type=jnp.float32)
    return joined.astype(jnp.bfloat16).reshape(tokens.shape[:-1] + (weight.shape[1],))


def attend(joined):
    length, batches = (joined.shape[0], joined.shape[1])
    inner_width = joined.shape[2] // 3
    head_count = inner_width // HEAD_DIM
    query_rows = joined[:, :, :inner_width].reshape(length, batches, head_count, HEAD_DIM)
    key_rows = joined[:, :, inner_width : 2 * inner_width].reshape(
        length, batches, head_count, HEAD_DIM
    )
    value_rows = joined[:, :, 2 * inner_width :].reshape(length, batches, head_count, HEAD_DIM)
    scores = jnp.einsum(
        "lbnd,mbnd->bnlm", query_rows, key_rows, preferred_element_type=jnp.float32
    ) * HEAD_DIM ** (-0.5)
    scores = scores - jnp.max(scores, axis=-1, keepdims=True)
    exponent = jnp.exp(scores)
    weights = (exponent / jnp.sum(exponent, axis=-1, keepdims=True)).astype(jnp.bfloat16)
    mixture = jnp.einsum("bnlm,mbnd->lbnd", weights, value_rows, preferred_element_type=jnp.float32)
    return mixture.reshape(length, batches, inner_width).astype(jnp.bfloat16)


def residual(tokens, mixture, weight):
    update = jnp.dot(
        mixture.reshape(-1, mixture.shape[-1]), weight, preferred_element_type=jnp.float32
    )
    return (tokens.astype(jnp.float32) + update.reshape(tokens.shape)).astype(jnp.bfloat16)


def frames_block(joined):
    length, single, places, triple = joined.shape
    mixture = attend(joined.reshape(length, single * places, triple))
    return mixture.reshape(length, single, places, triple // 3)


def plain_device(latents, qkv_weight, out_weight):
    frames_dev, rows_dev, columns, feature_width = latents.shape
    frame_count = lax.axis_size("frame")
    rows_attend = jax.vmap(attend)
    rows_att = rows_attend(
        project(
            lax.all_to_all(latents, "height", split_axis=2, concat_axis=1, tiled=True),
            qkv_weight[0],
        )
    )
    rows_att = lax.all_to_all(rows_att, "height", split_axis=1, concat_axis=2, tiled=True)
    middle = residual(latents, rows_att, out_weight[0])
    places_dev = rows_dev * columns // frame_count
    grouped = middle.reshape(frames_dev, frame_count, places_dev, feature_width)
    frames_att = frames_block(
        project(
            lax.all_to_all(grouped, "frame", split_axis=1, concat_axis=0, tiled=True), qkv_weight[1]
        )
    )
    frames_att = lax.all_to_all(frames_att, "frame", split_axis=0, concat_axis=1, tiled=True)
    frames_att = frames_att.reshape(frames_dev, rows_dev, columns, frames_att.shape[-1])
    return residual(middle, frames_att, out_weight[1])


VMEM = pl.BlockSpec(memory_space=pltpu.VMEM)
SMEM = pl.BlockSpec(memory_space=pltpu.SMEM)
ANY = pl.BlockSpec(memory_space=pl.ANY)


def split_kernel(count, place_ref, latents_ref, *refs):
    out_refs, sems = refs[:count], refs[count]
    width = out_refs[0].shape[1]
    copies = []
    for step in range(count):
        start = pl.multiple_of((place_ref[1] ^ step) * width, width)
        copies.append(
            pltpu.make_async_copy(
                latents_ref.at[0, :, pl.ds(start, width), :], out_refs[step], sems.at[step]
            )
        )
    for copy in copies:
        copy.start()
    for copy in copies:
        copy.wait()


def attend_kernel(count, group, *refs):
    block_refs, weight_ref = refs[:count], refs[count]
    out_refs = refs[count + 1 : 2 * count + 1]
    query_ref, key_ref, value_ref, mix_ref = refs[2 * count + 1 :]
    rows, batch, width = block_refs[0].shape
    inner = out_refs[0].shape[-1]
    length = count * rows
    tokens = length * group
    joined = []
    flat = jnp.concatenate([ref[...].reshape(rows * batch, width) for ref in block_refs], axis=0)
    joined = jnp.dot(layer_norm(flat), weight_ref[...], preferred_element_type=jnp.float32)
    joined = joined.reshape(length, batch, 3 * inner)
    first = lax.broadcasted_iota(jnp.int32, (tokens, tokens), 0) % group
    second = lax.broadcasted_iota(jnp.int32, (tokens, tokens), 1) % group
    same = first == second
    lane = lax.broadcasted_iota(jnp.int32, (tokens, WINDOW), 1)
    for number in range(batch // group):
        part = joined[:, number * group : (number + 1) * group].reshape(tokens, 3 * inner)
        part = part.astype(jnp.bfloat16)
        query_ref[:, :inner] = part[:, :inner]
        key_ref[:, :inner] = part[:, inner : 2 * inner]
        value_ref[:, :inner] = part[:, 2 * inner :]
        mix_ref[...] = jnp.zeros_like(mix_ref)
        for head in range(inner // HEAD_DIM):
            base = head * HEAD_DIM // LANES * LANES
            low = head * HEAD_DIM - base
            mine = (lane >= low) & (lane < low + HEAD_DIM)
            window = slice(base, base + WINDOW)
            query = jnp.where(mine, query_ref[:, window], 0)
            key = jnp.where(mine, key_ref[:, window], 0)
            value = jnp.where(mine, value_ref[:, window], 0)
            scores = lax.dot_general(
                query, key, (((1,), (1,)), ((), ())), preferred_element_type=jnp.float32
            ) * HEAD_DIM ** (-0.5)
            scores = jnp.where(same, scores, -jnp.inf)
            scores = scores - jnp.max(scores, axis=-1, keepdims=True)
            exponent = jnp.exp(scores)
            total = jnp.sum(exponent, axis=-1, keepdims=True)
            weights = (exponent / total).astype(jnp.bfloat16)
            mix_ref[:, window] += jnp.dot(weights, value, preferred_element_type=jnp.float32)
        mixture = mix_ref[:, :inner].reshape(length, group, inner).astype(jnp.bfloat16)
        for step in range(count):
            out_refs[step][:, number * group : (number + 1) * group, :] = mixture[
                step * rows : (step + 1) * rows
            ]


def middle_kernel(heights, frames, place_ref, *refs):
    token_refs, mix_refs = refs[:heights], refs[heights : 2 * heights]
    weight_ref = refs[2 * heights]
    out_refs = refs[2 * heights + 1 : -1]
    hold_ref = refs[-1]
    rows, columns, width = token_refs[0].shape
    per_block = rows * columns
    for step in range(heights):
        mixture = mix_refs[step][...].reshape(per_block, -1)
        update = jnp.dot(mixture, weight_ref[...], preferred_element_type=jnp.float32)
        tokens = token_refs[step][...].reshape(per_block, width).astype(jnp.float32)
        hold_ref[step * per_block : (step + 1) * per_block, :] = (tokens + update).astype(
            jnp.bfloat16
        )
    places = heights * per_block // frames
    for step in range(frames):
        start = pl.multiple_of((place_ref[0] ^ step) * places, places)
        out_refs[step][...] = hold_ref[pl.ds(start, places), :]


def result_kernel(frames, heights, place_ref, *refs):
    token_refs, mix_refs = refs[:frames], refs[frames : 2 * frames]
    weight_ref, out_ref = refs[2 * frames], refs[2 * frames + 1]
    places, width = token_refs[0].shape
    rows, columns = out_ref.shape[1], out_ref.shape[2] // heights
    for step in range(frames):
        update = jnp.dot(mix_refs[step][...], weight_ref[...], preferred_element_type=jnp.float32)
        block = (token_refs[step][...].astype(jnp.float32) + update).astype(jnp.bfloat16)
        start = (place_ref[0] ^ step) * places
        source = start // (rows * columns)
        row = (start - source * rows * columns) // columns
        column = pl.multiple_of((place_ref[1] ^ source) * columns, columns)
        for line in range(places // columns):
            out_ref[0, row + line, pl.ds(column, columns), :] = block[
                line * columns : (line + 1) * columns
            ]


def shaped(*shape, dtype=jnp.bfloat16):
    return jax.ShapeDtypeStruct(shape, dtype)


def attention(blocks, weight, group, name):
    count = len(blocks)
    rows, batch, width = blocks[0].shape
    inner = weight.shape[1] // 3
    padded = inner // LANES * LANES + WINDOW
    tokens = count * rows * group
    return pl.pallas_call(
        functools.partial(attend_kernel, count, group),
        out_shape=[shaped(rows, batch, inner)] * count,
        in_specs=[VMEM] * (count + 1),
        out_specs=[VMEM] * count,
        scratch_shapes=[pltpu.VMEM((tokens, padded), jnp.bfloat16)] * 3
        + [pltpu.VMEM((tokens, padded), jnp.float32)],
        name=name,
    )(*blocks, weight)


def swap(blocks, axis):
    count = len(blocks)
    out = [blocks[0]] + [None] * (count - 1)
    for step in reversed(range(1, count)):
        out[step] = lax.ppermute(blocks[step], axis, [(i, i ^ step) for i in range(count)])
    return out


def kernel_device(latents, qkv_weight, out_weight):
    frames_dev, rows, columns, width = latents.shape
    frames, heights = lax.axis_size("frame"), lax.axis_size("height")
    inner = out_weight.shape[1]
    place = jnp.stack([lax.axis_index("frame"), lax.axis_index("height")]).astype(jnp.int32)
    columns_dev = columns // heights
    places = rows * columns // frames
    mine = pl.pallas_call(
        functools.partial(split_kernel, heights),
        out_shape=[shaped(rows, columns_dev, width)] * heights,
        in_specs=[SMEM, ANY],
        out_specs=[VMEM] * heights,
        scratch_shapes=[pltpu.SemaphoreType.DMA((heights,))],
        name="split",
    )(place, latents)
    mix = attention(swap(mine, "height"), qkv_weight[0], 8, "row_attention")
    mix = swap(mix, "height")
    middle = pl.pallas_call(
        functools.partial(middle_kernel, heights, frames),
        out_shape=[shaped(places, width)] * frames,
        in_specs=[SMEM] + [VMEM] * (2 * heights + 1),
        out_specs=[VMEM] * frames,
        scratch_shapes=[pltpu.VMEM((rows * columns, width), jnp.bfloat16)],
        name="middle",
    )(place, *mine, *mix, out_weight[0])
    blocks = [block.reshape(1, places, width) for block in swap(middle, "frame")]
    mix = attention(blocks, qkv_weight[1], 24, "frame_attention")
    mix = swap([block.reshape(places, inner) for block in mix], "frame")
    return pl.pallas_call(
        functools.partial(result_kernel, frames, heights),
        out_shape=shaped(1, rows, columns, width),
        in_specs=[SMEM] + [VMEM] * (2 * frames + 1),
        out_specs=VMEM,
        name="result",
    )(place, *middle, *mix, out_weight[1])


def fits(shape, frames, heights):
    frames_dev, rows, columns, width = shape
    if frames & (frames - 1) or heights & (heights - 1) or frames_dev != 1 or frames > 8:
        return False
    columns_dev, places = columns // heights, rows * columns // frames
    return (
        columns_dev % 16 == 0
        and places % 48 == 0
        and places % columns_dev == 0
        and (rows * columns_dev) % places == 0
        and width % LANES == 0
    )


def per_device(latents, qkv_weight, out_weight):
    if fits(latents.shape, lax.axis_size("frame"), lax.axis_size("height")):
        return kernel_device(latents, qkv_weight, out_weight)
    return plain_device(latents, qkv_weight, out_weight)


def solution(mesh):
    return jax.shard_map(
        per_device,
        mesh=mesh,
        in_specs=(P("frame", "height", None, None), P(), P()),
        out_specs=P("frame", "height", None, None),
        check_vma=False,
    )
```

```python
import functools

import jax
import jax.numpy as jnp
from jax import lax
from jax.experimental import pallas as pl
from jax.experimental.pallas import tpu as pltpu
from jax.sharding import PartitionSpec as P

HEAD_DIM = 72
LANES = 128
WINDOW = 256


def layer_norm(values):
    values = values.astype(jnp.float32)
    center = values - jnp.mean(values, axis=-1, keepdims=True)
    spread = jnp.mean(center * center, axis=-1, keepdims=True)
    return (center * lax.rsqrt(spread + 1e-06)).astype(jnp.bfloat16)


def project(tokens, weight):
    normed = layer_norm(tokens)
    flattened = normed.reshape(-1, normed.shape[-1])
    joined = jnp.dot(flattened, weight, preferred_element_type=jnp.float32)
    return joined.astype(jnp.bfloat16).reshape(tokens.shape[:-1] + (weight.shape[1],))


def attend(joined):
    length, batches = (joined.shape[0], joined.shape[1])
    inner_width = joined.shape[2] // 3
    head_count = inner_width // HEAD_DIM
    query_rows = joined[:, :, :inner_width].reshape(length, batches, head_count, HEAD_DIM)
    key_rows = joined[:, :, inner_width : 2 * inner_width].reshape(
        length, batches, head_count, HEAD_DIM
    )
    value_rows = joined[:, :, 2 * inner_width :].reshape(length, batches, head_count, HEAD_DIM)
    scores = jnp.einsum(
        "lbnd,mbnd->bnlm", query_rows, key_rows, preferred_element_type=jnp.float32
    ) * HEAD_DIM ** (-0.5)
    scores = scores - jnp.max(scores, axis=-1, keepdims=True)
    exponent = jnp.exp(scores)
    weights = (exponent / jnp.sum(exponent, axis=-1, keepdims=True)).astype(jnp.bfloat16)
    mixture = jnp.einsum("bnlm,mbnd->lbnd", weights, value_rows, preferred_element_type=jnp.float32)
    return mixture.reshape(length, batches, inner_width).astype(jnp.bfloat16)


def residual(tokens, mixture, weight):
    update = jnp.dot(
        mixture.reshape(-1, mixture.shape[-1]), weight, preferred_element_type=jnp.float32
    )
    return (tokens.astype(jnp.float32) + update.reshape(tokens.shape)).astype(jnp.bfloat16)


def frames_block(joined):
    length, single, places, triple = joined.shape
    mixture = attend(joined.reshape(length, single * places, triple))
    return mixture.reshape(length, single, places, triple // 3)


def plain_device(latents, qkv_weight, out_weight):
    frames_dev, rows_dev, columns, feature_width = latents.shape
    frame_count = lax.axis_size("frame")
    rows_attend = jax.vmap(attend)
    rows_att = rows_attend(
        project(
            lax.all_to_all(latents, "height", split_axis=2, concat_axis=1, tiled=True),
            qkv_weight[0],
        )
    )
    rows_att = lax.all_to_all(rows_att, "height", split_axis=1, concat_axis=2, tiled=True)
    middle = residual(latents, rows_att, out_weight[0])
    places_dev = rows_dev * columns // frame_count
    grouped = middle.reshape(frames_dev, frame_count, places_dev, feature_width)
    frames_att = frames_block(
        project(
            lax.all_to_all(grouped, "frame", split_axis=1, concat_axis=0, tiled=True), qkv_weight[1]
        )
    )
    frames_att = lax.all_to_all(frames_att, "frame", split_axis=0, concat_axis=1, tiled=True)
    frames_att = frames_att.reshape(frames_dev, rows_dev, columns, frames_att.shape[-1])
    return residual(middle, frames_att, out_weight[1])


VMEM = pl.BlockSpec(memory_space=pltpu.VMEM)
ANY = pl.BlockSpec(memory_space=pl.ANY)


def split_kernel(count, latents_ref, *refs):
    out_refs, sems = refs[:count], refs[count]
    width = out_refs[0].shape[1]
    copies = []
    for step in range(count):
        start = pl.multiple_of((lax.axis_index("height") ^ step) * width, width)
        copies.append(
            pltpu.make_async_copy(
                latents_ref.at[0, :, pl.ds(start, width), :], out_refs[step], sems.at[step]
            )
        )
    for copy in copies:
        copy.start()
    for copy in copies:
        copy.wait()


def fetch_kernel(count, *refs):
    copies = [
        pltpu.make_async_copy(refs[i], refs[count + i], refs[-1].at[i]) for i in range(count)
    ]
    for copy in copies:
        copy.start()
    for copy in copies:
        copy.wait()


def attend_kernel(count, group, half, *refs):
    block_refs, weight_ref = refs[:count], refs[count]
    out_refs = refs[count + 1 : 2 * count + 1]
    query_ref, key_ref, value_ref, mix_ref = refs[2 * count + 1 :]
    rows, batch, width = block_refs[0].shape
    inner = out_refs[0].shape[-1]
    length = count * rows
    tokens = length * group
    flat = jnp.concatenate([ref[...].reshape(rows * batch, width) for ref in block_refs], axis=0)
    joined = lax.dot_general(
        layer_norm(flat),
        weight_ref[half],
        (((1,), (1,)), ((), ())),
        preferred_element_type=jnp.float32,
    )
    joined = joined.reshape(length, batch, 3 * inner)
    first = lax.broadcasted_iota(jnp.int32, (tokens, tokens), 0) % group
    second = lax.broadcasted_iota(jnp.int32, (tokens, tokens), 1) % group
    same = first == second
    lane = lax.broadcasted_iota(jnp.int32, (tokens, WINDOW), 1)
    for number in range(batch // group):
        part = joined[:, number * group : (number + 1) * group].reshape(tokens, 3 * inner)
        part = part.astype(jnp.bfloat16)
        query_ref[:, :inner] = part[:, :inner]
        key_ref[:, :inner] = part[:, inner : 2 * inner]
        value_ref[:, :inner] = part[:, 2 * inner :]
        mix_ref[...] = jnp.zeros_like(mix_ref)
        for head in range(inner // HEAD_DIM):
            base = head * HEAD_DIM // LANES * LANES
            low = head * HEAD_DIM - base
            mine = (lane >= low) & (lane < low + HEAD_DIM)
            window = slice(base, base + WINDOW)
            query = jnp.where(mine, query_ref[:, window], 0)
            key = jnp.where(mine, key_ref[:, window], 0)
            value = jnp.where(mine, value_ref[:, window], 0)
            scores = lax.dot_general(
                query, key, (((1,), (1,)), ((), ())), preferred_element_type=jnp.float32
            ) * HEAD_DIM ** (-0.5)
            scores = jnp.where(same, scores, -jnp.inf)
            scores = scores - jnp.max(scores, axis=-1, keepdims=True)
            exponent = jnp.exp(scores)
            total = jnp.sum(exponent, axis=-1, keepdims=True)
            weights = (exponent / total).astype(jnp.bfloat16)
            mix_ref[:, window] += jnp.dot(weights, value, preferred_element_type=jnp.float32)
        mixture = mix_ref[:, :inner].reshape(length, group, inner).astype(jnp.bfloat16)
        for step in range(count):
            out_refs[step][:, number * group : (number + 1) * group, :] = mixture[
                step * rows : (step + 1) * rows
            ]


def middle_kernel(heights, frames, *refs):
    token_refs, mix_refs = refs[:heights], refs[heights : 2 * heights]
    weight_ref = refs[2 * heights]
    out_refs = refs[2 * heights + 1 : -1]
    hold_ref = refs[-1]
    rows, columns, width = token_refs[0].shape
    per_block = rows * columns
    mixture = jnp.concatenate([ref[...].reshape(per_block, -1) for ref in mix_refs], axis=0)
    tokens = jnp.concatenate([ref[...].reshape(per_block, width) for ref in token_refs], axis=0)
    update = jnp.dot(mixture, weight_ref[0], preferred_element_type=jnp.float32)
    hold_ref[...] = (tokens.astype(jnp.float32) + update).astype(jnp.bfloat16)
    places = heights * per_block // frames
    for step in range(frames):
        start = pl.multiple_of((lax.axis_index("frame") ^ step) * places, places)
        out_refs[step][...] = hold_ref[pl.ds(start, places), :]


def result_kernel(frames, heights, *refs):
    token_refs, mix_refs = refs[:frames], refs[frames : 2 * frames]
    weight_ref, out_ref = refs[2 * frames], refs[2 * frames + 1]
    places, _ = token_refs[0].shape
    rows, columns = out_ref.shape[1], out_ref.shape[2] // heights
    mixture = jnp.concatenate([ref[...] for ref in mix_refs], axis=0)
    tokens = jnp.concatenate([ref[...] for ref in token_refs], axis=0)
    update = jnp.dot(mixture, weight_ref[1], preferred_element_type=jnp.float32)
    result = (tokens.astype(jnp.float32) + update).astype(jnp.bfloat16)
    for step in range(frames):
        block = result[step * places : (step + 1) * places]
        start = (lax.axis_index("frame") ^ step) * places
        source = start // (rows * columns)
        row = (start - source * rows * columns) // columns
        column = pl.multiple_of((lax.axis_index("height") ^ source) * columns, columns)
        for line in range(places // columns):
            out_ref[0, row + line, pl.ds(column, columns), :] = block[
                line * columns : (line + 1) * columns
            ]


def shaped(*shape, dtype=jnp.bfloat16):
    return pltpu.VMEM(shape, dtype)


def near(arrays):
    return [pltpu.with_memory_space_constraint(array, pltpu.VMEM) for array in arrays]


PARAMS = pltpu.CompilerParams(vmem_limit_bytes=24 * 2**20)


def attention(blocks, weight, group, half):
    count = len(blocks)
    rows, batch, _ = blocks[0].shape
    inner = weight.shape[1] // 3
    padded = inner // LANES * LANES + WINDOW
    tokens = count * rows * group
    return pl.pallas_call(
        functools.partial(attend_kernel, count, group, half),
        out_shape=[shaped(rows, batch, inner)] * count,
        in_specs=[VMEM] * (count + 1),
        out_specs=[VMEM] * count,
        scratch_shapes=[pltpu.VMEM((tokens, padded), jnp.bfloat16)] * 3
        + [pltpu.VMEM((tokens, padded), jnp.float32)],
        compiler_params=PARAMS,
    )(*near(blocks), weight)


def swap(blocks, axis):
    count = len(blocks)
    out = [blocks[0]] + [None] * (count - 1)
    for step in range(1, count):
        out[step] = lax.ppermute(blocks[step], axis, [(i, i ^ step) for i in range(count)])
    return out


def kernel_device(latents, qkv_weight, out_weight):
    _, rows, columns, width = latents.shape
    frames, heights = lax.axis_size("frame"), lax.axis_size("height")
    inner = out_weight.shape[1]
    qkv_weight = jnp.swapaxes(qkv_weight, 1, 2)
    qkv_weight, out_weight = pl.pallas_call(
        functools.partial(fetch_kernel, 2),
        out_shape=[shaped(*qkv_weight.shape), shaped(*out_weight.shape)],
        in_specs=[ANY] * 2,
        out_specs=[VMEM] * 2,
        scratch_shapes=[pltpu.SemaphoreType.DMA((2,))],
        compiler_params=PARAMS,
        cost_estimate=pl.CostEstimate(flops=0, transcendentals=0, bytes_accessed=2 * 10**7),
        name="fetch",
    )(qkv_weight, out_weight)
    qkv_weight, out_weight = near([qkv_weight, out_weight])
    columns_dev = columns // heights
    places = rows * columns // frames
    mine = pl.pallas_call(
        functools.partial(split_kernel, heights),
        out_shape=[shaped(rows, columns_dev, width)] * heights,
        in_specs=[ANY],
        out_specs=[VMEM] * heights,
        scratch_shapes=[pltpu.SemaphoreType.DMA((heights,))],
        name="split",
    )(latents)
    mix = attention(swap(mine, "height"), qkv_weight, 8, 0)
    mix = swap(mix, "height")
    middle = pl.pallas_call(
        functools.partial(middle_kernel, heights, frames),
        out_shape=[shaped(places, width)] * frames,
        in_specs=[VMEM] * (2 * heights + 1),
        out_specs=[VMEM] * frames,
        scratch_shapes=[pltpu.VMEM((rows * columns, width), jnp.bfloat16)],
        compiler_params=PARAMS,
        name="middle",
    )(*near(mine), *near(mix), out_weight)
    blocks = [block.reshape(1, places, width) for block in swap(middle, "frame")]
    mix = attention(blocks, qkv_weight, 24, 1)
    mix = swap([block.reshape(places, inner) for block in mix], "frame")
    return pl.pallas_call(
        functools.partial(result_kernel, frames, heights),
        out_shape=jax.ShapeDtypeStruct((1, rows, columns, width), jnp.bfloat16),
        in_specs=[VMEM] * (2 * frames + 1),
        out_specs=VMEM,
        compiler_params=PARAMS,
        name="result",
    )(*near(middle), *near(mix), out_weight)


def fits(shape, frames, heights):
    frames_dev, rows, columns, width = shape
    if frames & (frames - 1) or heights & (heights - 1) or frames_dev != 1 or frames > 8:
        return False
    columns_dev, places = columns // heights, rows * columns // frames
    return (
        columns_dev % 16 == 0
        and places % 48 == 0
        and places % columns_dev == 0
        and (rows * columns_dev) % places == 0
        and width % LANES == 0
    )


def solution(mesh):
    def per_device(latents, qkv_weight, out_weight):
        if fits(latents.shape, mesh.shape["frame"], mesh.shape["height"]):
            return kernel_device(latents, qkv_weight, out_weight)
        return plain_device(latents, qkv_weight, out_weight)

    return jax.shard_map(
        per_device,
        mesh=mesh,
        in_specs=(P("frame", "height", None, None), P(), P()),
        out_specs=P("frame", "height", None, None),
        check_vma=False,
    )
```
